512 devices in a mesh: gx: 32 (over z, x), gy: 16 (over y, core).
Axes of the slice: x: 4, y: 8, z: 8, core: 2. Of those that a mesh axis runs over, the one named last changes fastest.
Arguments:
- source: float32 [2048, 256, 128], P('gx', 'gy'), may hold values from -5 to 5
Outputs:
- pressure: float32 [2048, 256, 128], P('gx', 'gy')
The draws below stay inside these ranges and needn't reach their ends.
All inputs are finite; a program needn't handle non-finite values.
Results may differ from the reference program's by a relative error of at most 0.0003.
Values sent between devices are 32-bit elements; how exact they have to be, the bound alone decides.
A program may use at most 64 MiB of HBM per device.

```python
import math
import jax
import jax.numpy as jnp
from jax import lax

NX = 2048
NZ = 128
NY = 256
SCREEN = 32


def draw_source(key, part):
    return jax.random.truncated_normal(key, -5.0, 5.0, (NX, NY, NZ), jnp.float32)


def setup_inputs(seed: int = 0) -> dict:
    keys = jax.random.split(jax.random.key(seed), 2)
    return {
        "source": draw_source(jax.random.fold_in(keys[1], 71), 0),
    }


highest = lax.Precision.HIGHEST

def cosine_table(points, wavenums, places):
    angles = wavenums[:, None] * (2 * places[None, :] + 1) % (4 * points)
    norming = jnp.where(wavenums == 0, math.sqrt(1.0 / points), math.sqrt(2.0 / points)).astype(jnp.float32)
    return norming[:, None] * jnp.cos(angles.astype(jnp.float32) * (math.pi / (2 * points)))

def eigenvalue(wavenums, points):
    half_angle = jnp.sin(wavenums.astype(jnp.float32) * (math.pi / (2 * points)))
    return 4.0 * half_angle * half_angle

def thomas(rhs_lines, diagonal):

    def forward_step(carry, source_line):
        factor, eliminated = carry
        factor = 1.0 / (diagonal - factor)
        eliminated = (source_line + eliminated) * factor
        return ((factor, eliminated), (factor, eliminated))
    empty_line = jnp.zeros_like(rhs_lines[0])
    unused, (factors, eliminated) = lax.scan(forward_step, (empty_line, empty_line), rhs_lines, unroll=8)

    def backward_step(pressure_next, inputs_line):
        solved_line = inputs_line[1] + inputs_line[0] * pressure_next
        return (solved_line, solved_line)
    unused_last, solution = lax.scan(backward_step, empty_line, (factors, eliminated), reverse=True, unroll=8)
    return solution

def reference(source):
    nz_waves = jnp.arange(NZ, dtype=jnp.int32)
    z_table = cosine_table(NZ, nz_waves, nz_waves)
    zhat = jnp.einsum('xyz,kz->xyk', source, z_table, precision=highest)
    x_places = jnp.arange(NX, dtype=jnp.int32)
    offsets = jnp.arange(NX // 128, dtype=jnp.int32) * 128

    def forward_block(offset):
        cos_table = cosine_table(NX, offset + jnp.arange(128, dtype=jnp.int32), x_places)
        return jnp.einsum('xyz,kx->kyz', zhat, cos_table, precision=highest)
    spectral = lax.map(forward_block, offsets).reshape(NX, NY, NZ)
    diagonal = 2.0 + (1.0 / (SCREEN * SCREEN) + eigenvalue(x_places, NX)[:, None] + eigenvalue(nz_waves, NZ)[None, :])
    solution = thomas(jnp.moveaxis(spectral, 1, 0), diagonal)

    def backward_block(offset):
        cos_table = cosine_table(NX, x_places, offset + jnp.arange(128, dtype=jnp.int32))
        return jnp.einsum('ykz,kx->xyz', solution, cos_table, precision=highest)
    physical = lax.map(backward_block, offsets).reshape(NX, NY, NZ)
    return jnp.einsum('xyk,kz->xyz', physical, z_table, precision=highest)
```

```python
import functools
import math

import jax
import jax.numpy as jnp
import ml_dtypes
import numpy as np
from jax import lax
from jax.experimental import pallas as pl
from jax.experimental.pallas import tpu as pltpu
from jax.sharding import PartitionSpec as P

SCREEN = 32
X_CHIPS = 8
CHUNKS = 2
MESH = pl.DeviceIdType.MESH
f32, bf16 = jnp.float32, jnp.bfloat16


def halves(table):
    high = table.astype(ml_dtypes.bfloat16)
    low = (table - high.astype(np.float64)).astype(ml_dtypes.bfloat16)
    return high, low


def z_tables(nz, gy):
    waves, places = np.arange(nz)[:, None], np.arange(nz)[None, :]
    norm = np.where(waves == 0, math.sqrt(1.0 / nz), math.sqrt(2.0 / nz))
    cosines = norm * np.cos(np.pi * ((waves * (2 * places + 1)) % (4 * nz)) / (2 * nz))
    group = nz // gy // CHUNKS
    blocks = cosines.reshape(gy, CHUNKS, group, nz)
    table = np.zeros((CHUNKS, gy, 2, group, 2, nz))
    for bit in range(2):
        table[:, :, bit, :, bit, :] = blocks.transpose(1, 0, 2, 3)
    return halves(table.reshape(CHUNKS, gy * 2 * group, 2 * nz))


def y_tables(ny, gy):
    line = np.arange(1, ny + 1)
    sines = math.sqrt(2.0 / (ny + 1)) * np.sin(
        np.pi * ((line[:, None] * line[None, :]) % (2 * (ny + 1))) / (ny + 1)
    )
    quads = sines.reshape(gy, ny // gy // 4, 2, 2, ny)
    return halves(quads.transpose(3, 2, 0, 1, 4).reshape(ny, ny))


def line_tables(ny, nz, gy):
    q, m = np.arange(ny), np.arange(nz)
    shift = (
        1.0 / (SCREEN * SCREEN)
        + 4.0 * np.sin(np.pi * (q[:, None] + 1) / (2 * (ny + 1))) ** 2
        + 4.0 * np.sin(np.pi * m[None, :] / (2 * nz)) ** 2
    )
    root = np.sqrt(shift * (1.0 + shift / 4.0))
    ratio = 1.0 / (1.0 + shift / 2.0 + root)
    both = np.stack([ratio, 0.5 / root])
    group = nz // gy // CHUNKS
    both = both.reshape(2, 2, ny // 2, gy, CHUNKS, group)
    both = both.transpose(3, 4, 0, 1, 5, 2)
    return both.reshape(gy, CHUNKS, 2, 2 * group, ny // 2).astype(np.float32)


def split(value):
    high = value.astype(bf16)
    return high, (value - high.astype(f32)).astype(bf16)


def product(left, right, dims):
    def dot(a, b):
        return lax.dot_general(a, b, (dims, ((), ())), preferred_element_type=f32)

    return dot(left[0], right[0]) + (dot(left[1], right[0]) + dot(left[0], right[1]))


def kernel(
    gx, gy, x_chips, lx, ly, nz, ny,
    f_ref, c_hi_hbm, c_lo_hbm, s_hi_hbm, s_lo_hbm, lines_hbm,
    o_ref,
    c_hi, c_lo, s_hi, s_lo, lines,
    g_hi, g_lo, out_fwd, in_fwd, wave, powers, sums_up, sums_down, solved, out_bwd, in_bwd, total,
    ends, ends_x, tops, tops_z,
    table_sem, fwd_send, fwd_recv, bwd_send, bwd_recv, x_send, x_recv, z_send, z_recv,
):
    z_chips, y_chips = gx // x_chips, gy // 2
    quads = ly // 4
    group = nz // gy // CHUNKS
    rows = 2 * group
    block = quads * rows
    half = gy * quads
    ql = ny // 2

    gxi, gyi = lax.axis_index("gx"), lax.axis_index("gy")
    zi, xi = gxi // x_chips, lax.rem(gxi, x_chips)
    yi, core = gyi // 2, lax.rem(gyi, 2)

    def y_peer(sign, dy, dc):
        chip = lax.rem(yi + sign * dy + y_chips, y_chips)
        return chip * 2 + lax.rem(core + dc, 2)

    order = sorted(range(y_chips), key=lambda d: (-min(d, y_chips - d), d))
    y_moves = [(dy, dc) for dy in order for dc in range(2) if (dy, dc) != (0, 0)]
    x_order = sorted(range(1, x_chips), key=lambda d: (-min(d, x_chips - d), d))

    def x_peer(sign, d):
        return zi * x_chips + lax.rem(xi + sign * d + x_chips, x_chips)

    def z_peer(sign, d):
        return lax.rem(zi + sign * d + z_chips, z_chips) * x_chips + xi

    barrier = pltpu.get_barrier_semaphore()
    for dy, dc in y_moves:
        pl.semaphore_signal(
            barrier, inc=1, device_id=(gxi, y_peer(1, dy, dc)), device_id_type=MESH
        )
    for d in x_order:
        pl.semaphore_signal(barrier, inc=1, device_id=(x_peer(1, d), gyi), device_id_type=MESH)
    for d in range(1, z_chips):
        pl.semaphore_signal(barrier, inc=1, device_id=(z_peer(1, d), gyi), device_id_type=MESH)

    loads = [
        pltpu.make_async_copy(source, target, table_sem.at[i])
        for i, (source, target) in enumerate(
            [
                (c_hi_hbm, c_hi),
                (c_lo_hbm, c_lo),
                (s_hi_hbm, s_hi),
                (s_lo_hbm, s_lo),
                (lines_hbm.at[gyi], lines),
            ]
        )
    ]
    for load in loads:
        load.start()

    for t in range(quads):
        cells = [[f_ref[pl.ds(4 * t + 2 * b1 + b0, lx, stride=ly), :] for b1 in range(2)]
                 for b0 in range(2)]
        spread = jnp.concatenate([jnp.concatenate(row, axis=1) for row in cells], axis=0)
        high, low = split(spread)
        g_hi[t] = high
        g_lo[t] = low
    for load in loads:
        load.wait()

    def block_of(index):
        return pl.ds(pl.multiple_of(index * block, block), block)

    def z_forward(c):
        for t in range(quads):
            piece = product((c_hi[c], c_lo[c]), (g_hi[t], g_lo[t]), ((1,), (1,)))
            for j in range(gy):
                out_fwd[c, j * block + t * rows : j * block + (t + 1) * rows, :] = piece[
                    j * rows : (j + 1) * rows, :
                ]

    def y_copies(c, out, into, send, recv):
        sends, arrivals = [], []
        for i, (dy, dc) in enumerate(y_moves):
            peer, source = y_peer(1, dy, dc), y_peer(-1, dy, dc)
            for copies, src, dst in ((sends, peer, gyi), (arrivals, source, source)):
                copies.append(
                    pltpu.make_async_remote_copy(
                        src_ref=out.at[c, block_of(src)],
                        dst_ref=into.at[c, block_of(dst)],
                        send_sem=send.at[c, i],
                        recv_sem=recv.at[c, i],
                        device_id=(gxi, peer),
                        device_id_type=MESH,
                    )
                )
        return sends, arrivals

    def exchange(c, out, into, send, recv):
        sends, arrivals = y_copies(c, out, into, send, recv)
        for copy in sends:
            copy.start()
        into[c, block_of(gyi), :] = out[c, block_of(gyi), :]
        return sends, arrivals

    z_forward(0)
    pl.semaphore_wait(barrier, len(y_moves) + x_chips - 1 + z_chips - 1)
    fwd = [exchange(0, out_fwd, in_fwd, fwd_send, fwd_recv)]
    for c in range(1, CHUNKS):
        z_forward(c)
        fwd.append(exchange(c, out_fwd, in_fwd, fwd_send, fwd_recv))

    for c in range(CHUNKS):
        ratio = lines[c, 0]
        power = jnp.ones_like(ratio)
        for b in range(lx):
            powers[c, b] = power
            power = power * ratio

    def y_forward(c):
        for copy in fwd[c][1]:
            copy.wait_recv()
        tall = []
        for m in range(group):
            cells = jnp.concatenate(
                [in_fwd[c, pl.ds(b1 * group + m, half, stride=rows), :] for b1 in range(2)], axis=0
            ).T
            tall.append(jnp.concatenate([cells[:lx], cells[lx:]], axis=1))
        spectral = product(split(jnp.concatenate(tall, axis=0)), (s_hi[...], s_lo[...]),
                           ((1,), (0,)))
        for h in range(2):
            wave[c, h * group * lx : (h + 1) * group * lx, :] = spectral[:, h * ql : (h + 1) * ql]

    def small_copies(c, out, into, slot, send, recv, distances, peer_of, source_slot):
        sends, arrivals = [], []
        for i, d in enumerate(distances):
            for copies, dst in ((sends, slot), (arrivals, source_slot(d))):
                copies.append(
                    pltpu.make_async_remote_copy(
                        src_ref=out.at[c],
                        dst_ref=into.at[c, dst],
                        send_sem=send.at[c, i],
                        recv_sem=recv.at[c, i],
                        device_id=(peer_of(1, d), gyi),
                        device_id_type=MESH,
                    )
                )
        return sends, arrivals

    def line(ref, c, b):
        return ref[c, pl.ds(b, rows, stride=lx), :]

    def x_ends(c):
        left = [jnp.zeros((rows, ql), f32) for _ in range(4)]
        right = list(left)
        for b in range(lx):
            value = line(wave, c, b)
            left[b % 4] += value * powers[c, b]
            right[b % 4] += value * powers[c, lx - 1 - b]
        ends[c, 0] = (left[0] + left[1]) + (left[2] + left[3])
        ends[c, 1] = (right[0] + right[1]) + (right[2] + right[3])
        sends, arrivals = small_copies(
            c, ends, ends_x, xi, x_send, x_recv, x_order, x_peer,
            lambda d: lax.rem(xi - d + x_chips, x_chips),
        )
        for copy in sends:
            copy.start()
        ends_x[c, xi] = ends[c]
        return sends, arrivals

    def x_local(c):
        ratio = lines[c, 0]
        up = jnp.zeros((rows, ql), f32)
        down = up
        for b in range(lx):
            up = ratio * up + line(wave, c, b)
            sums_up[c, b] = up
            d = lx - 1 - b
            down = ratio * down
            sums_down[c, d] = down
            down = down + line(wave, c, d)

    def x_group(c, copies):
        for copy in copies[1]:
            copy.wait_recv()
        span = powers[c, lx - 1] * lines[c, 0]
        left = ends_x[c, x_chips - 1, 0]
        right = ends_x[c, 0, 1]
        for i in range(1, x_chips):
            left = span * left + ends_x[c, x_chips - 1 - i, 0]
            right = span * right + ends_x[c, i, 1]
        tops[c, 0] = left
        tops[c, 1] = right
        sends, arrivals = small_copies(
            c, tops, tops_z, zi, z_send, z_recv, range(1, z_chips), z_peer,
            lambda d: lax.rem(zi - d + z_chips, z_chips),
        )
        for copy in sends:
            copy.start()
        tops_z[c, zi] = tops[c]
        return sends, arrivals

    def arriving(span, count, place, parts, left_start, right_start):
        right = right_start
        left = left_start
        for i in range(count):
            left = jnp.where(i < place, span * left + parts(i, 1), left)
            o = count - 1 - i
            right = jnp.where(o > place, span * right + parts(o, 0), right)
        return left, right

    def x_finish(c, copies):
        ratio, scale = lines[c, 0], lines[c, 1]
        span = powers[c, lx - 1] * ratio
        wide = span
        for _ in range(x_chips - 1):
            wide = wide * span
        whole = wide
        for _ in range(z_chips - 1):
            whole = whole * wide
        for copy in copies[1]:
            copy.wait_recv()
        left = tops_z[c, z_chips - 1, 0]
        right = tops_z[c, 0, 1]
        for i in range(1, z_chips):
            left = wide * left + tops_z[c, z_chips - 1 - i, 0]
            right = wide * right + tops_z[c, i, 1]
        closing = 1.0 / (1.0 - whole * whole)
        first = (left + whole * right) * closing
        last = (right + whole * left) * closing
        first, last = arriving(wide, z_chips, zi, lambda i, s: tops_z[c, i, s], first, last)
        first, last = arriving(span, x_chips, xi, lambda i, s: ends_x[c, i, s], first, last)
        first = first * (ratio * scale)
        last = last * (ratio * scale)
        for b in range(lx):
            solved[c, pl.ds(b, rows, stride=lx), :] = (
                scale * (sums_up[c, b] + sums_down[c, b])
                + first * powers[c, b]
                + last * powers[c, lx - 1 - b]
            )

    def y_backward(c):
        flat = group * lx
        lanes = jnp.concatenate([solved[c, h * flat : (h + 1) * flat, :] for h in range(2)], axis=1)
        cells = product(split(lanes), (s_hi[...], s_lo[...]), ((1,), (1,)))
        for m in range(group):
            part = cells[m * lx : (m + 1) * lx]
            part = jnp.concatenate([part[:, : ny // 2], part[:, ny // 2 :]], axis=0).T
            for b1 in range(2):
                out_bwd[c, pl.ds(b1 * group + m, half, stride=rows), :] = part[
                    b1 * half : (b1 + 1) * half
                ]
        return exchange(c, out_bwd, in_bwd, bwd_send, bwd_recv)

    def z_backward(c, copies):
        for copy in copies[1]:
            copy.wait_recv()
        for t in range(quads):
            waves = jnp.concatenate(
                [in_bwd[c, j * block + t * rows : j * block + (t + 1) * rows, :]
                 for j in range(gy)], axis=0,
            ).T
            cells = product(split(waves), (c_hi[c], c_lo[c]), ((1,), (0,)))
            if c > 0:
                cells = cells + total[t]
            if c < CHUNKS - 1:
                total[t] = cells
            else:
                for b0 in range(2):
                    for b1 in range(2):
                        o_ref[pl.ds(4 * t + 2 * b1 + b0, lx, stride=ly), :] = cells[
                            b0 * lx : (b0 + 1) * lx, b1 * nz : (b1 + 1) * nz
                        ]

    assert CHUNKS == 2
    y_forward(0)
    x_copies = [x_ends(0)]
    x_local(0)
    y_forward(1)
    x_copies.append(x_ends(1))
    z_copies = [x_group(0, x_copies[0])]
    x_local(1)
    x_finish(0, z_copies[0])
    bwd = [y_backward(0)]
    z_copies.append(x_group(1, x_copies[1]))
    x_finish(1, z_copies[1])
    bwd.append(y_backward(1))
    z_backward(0, bwd[0])
    z_backward(1, bwd[1])
    for sends, _ in fwd + x_copies + z_copies + bwd:
        for copy in sends:
            copy.wait_send()


def solve(gx, gy, x_chips, source):
    lx, ly, nz = source.shape
    ny = ly * gy
    z_chips = gx // x_chips
    group = nz // gy // CHUNKS
    rows, ql = 2 * group, ny // 2
    c_hi, c_lo = z_tables(nz, gy)
    s_hi, s_lo = y_tables(ny, gy)
    lines = line_tables(ny, nz, gy)
    buffer = pltpu.VMEM((CHUNKS, gy * (ly // 4) * rows, 2 * lx), f32)
    spectral = pltpu.VMEM((CHUNKS, rows * lx, ql), f32)
    stack = pltpu.VMEM((CHUNKS, lx, rows, ql), f32)
    quad = pltpu.VMEM((ly // 4, 2 * lx, 2 * nz), bf16)
    dma = pltpu.SemaphoreType.DMA
    scratch = [
        pltpu.VMEM(c_hi.shape, bf16), pltpu.VMEM(c_lo.shape, bf16),
        pltpu.VMEM(s_hi.shape, bf16), pltpu.VMEM(s_lo.shape, bf16),
        pltpu.VMEM(lines.shape[1:], f32),
        quad, quad, buffer, buffer, spectral, stack, stack, stack, spectral, buffer, buffer,
        pltpu.VMEM((ly // 4, 2 * lx, 2 * nz), f32),
        pltpu.VMEM((CHUNKS, 2, rows, ql), f32),
        pltpu.VMEM((CHUNKS, x_chips, 2, rows, ql), f32),
        pltpu.VMEM((CHUNKS, 2, rows, ql), f32),
        pltpu.VMEM((CHUNKS, z_chips, 2, rows, ql), f32),
        dma((5,)),
        dma((CHUNKS, gy - 1)), dma((CHUNKS, gy - 1)), dma((CHUNKS, gy - 1)), dma((CHUNKS, gy - 1)),
        dma((CHUNKS, x_chips - 1)), dma((CHUNKS, x_chips - 1)),
        dma((CHUNKS, z_chips - 1)), dma((CHUNKS, z_chips - 1)),
    ]
    vmem, anywhere = pl.BlockSpec(memory_space=pltpu.VMEM), pl.BlockSpec(memory_space=pl.ANY)
    pressure = pl.pallas_call(
        functools.partial(kernel, gx, gy, x_chips, lx, ly, nz, ny),
        out_shape=jax.ShapeDtypeStruct((lx * ly, nz), f32),
        in_specs=[vmem] + [anywhere] * 5,
        out_specs=vmem,
        scratch_shapes=scratch,
        compiler_params=pltpu.CompilerParams(collective_id=0, has_side_effects=True),
    )(source.reshape(lx * ly, nz), c_hi, c_lo, s_hi, s_lo, lines)
    return pressure.reshape(lx, ly, nz)


def solution(mesh):
    gx, gy = mesh.shape["gx"], mesh.shape["gy"]
    return jax.shard_map(
        functools.partial(solve, gx, gy, X_CHIPS),
        mesh=mesh,
        in_specs=(P("gx", "gy", None),),
        out_specs=P("gx", "gy", None),
        check_vma=False,
    )
```

```python
import functools
import math

import jax
import jax.numpy as jnp
import ml_dtypes
import numpy as np
from jax import lax
from jax.experimental import pallas as pl
from jax.experimental.pallas import tpu as pltpu
from jax.sharding import PartitionSpec as P

SCREEN = 32
X_CHIPS = 8
CHUNKS = 4
TILE = 8
MESH = pl.DeviceIdType.MESH
f32, bf16 = jnp.float32, jnp.bfloat16


def halves(table):
    high = table.astype(ml_dtypes.bfloat16)
    low = (table - high.astype(np.float64)).astype(ml_dtypes.bfloat16)
    return high, low


def z_tables(nz, gy):
    waves, places = np.arange(nz)[:, None], np.arange(nz)[None, :]
    norm = np.where(waves == 0, math.sqrt(1.0 / nz), math.sqrt(2.0 / nz))
    cosines = norm * np.cos(np.pi * ((waves * (2 * places + 1)) % (4 * nz)) / (2 * nz))
    group = nz // gy // CHUNKS
    sub = TILE // group
    blocks = cosines.reshape(gy, CHUNKS, group, nz)
    table = np.zeros((CHUNKS, gy, sub, group, sub, nz))
    for s in range(sub):
        table[:, :, s, :, s, :] = blocks.transpose(1, 0, 2, 3)
    return halves(table.reshape(CHUNKS, gy * TILE, sub * nz))


def y_tables(ny, gy, sub):
    line = np.arange(1, ny + 1)
    sines = math.sqrt(2.0 / (ny + 1)) * np.sin(
        np.pi * ((line[:, None] * line[None, :]) % (2 * (ny + 1))) / (ny + 1)
    )
    cells = sines.reshape(gy, ny // gy // (2 * sub), sub, 2, ny)
    return halves(cells.transpose(3, 2, 0, 1, 4).reshape(ny, ny))


def line_tables(ny, nz, gy):
    q, m = np.arange(ny), np.arange(nz)
    shift = (
        1.0 / (SCREEN * SCREEN)
        + 4.0 * np.sin(np.pi * (q[:, None] + 1) / (2 * (ny + 1))) ** 2
        + 4.0 * np.sin(np.pi * m[None, :] / (2 * nz)) ** 2
    )
    root = np.sqrt(shift * (1.0 + shift / 4.0))
    ratio = 1.0 / (1.0 + shift / 2.0 + root)
    both = np.stack([ratio, 0.5 / root])
    group = nz // gy // CHUNKS
    both = both.reshape(2, 2, ny // 2, gy, CHUNKS, group)
    both = both.transpose(3, 4, 0, 1, 5, 2)
    return both.reshape(gy, CHUNKS, 2, 2 * group, ny // 2).astype(np.float32)


def split(value):
    high = value.astype(bf16)
    return high, (value - high.astype(f32)).astype(bf16)


def product(left, right, dims):
    def dot(a, b):
        return lax.dot_general(a, b, (dims, ((), ())), preferred_element_type=f32)

    return dot(left[0], right[0]) + (dot(left[1], right[0]) + dot(left[0], right[1]))


def kernel(
    gx, gy, x_chips, lx, ly, nz, ny,
    f_hbm, c_hi_hbm, c_lo_hbm, s_hi_hbm, s_lo_hbm, lines_hbm,
    o_ref,
    f_ref, c_hi, c_lo, s_hi, s_lo, lines,
    g_hi, g_lo, out_fwd, in_fwd, wave, powers, sums_up, sums_down, solved, out_bwd, in_bwd, total,
    ends, ends_x, tops, tops_z,
    table_sem, fwd_send, fwd_recv, bwd_send, bwd_recv, x_send, x_recv, z_send, z_recv,
):
    z_chips, y_chips = gx // x_chips, gy // 2
    group = nz // gy // CHUNKS
    sub = TILE // group
    steps = ly // (2 * sub)
    rows = 2 * group
    block = steps * TILE
    part = gy * steps
    ql = ny // 2

    gxi, gyi = lax.axis_index("gx"), lax.axis_index("gy")
    zi, xi = gxi // x_chips, lax.rem(gxi, x_chips)
    yi, core = gyi // 2, lax.rem(gyi, 2)

    def y_peer(sign, dy, dc):
        chip = lax.rem(yi + sign * dy + y_chips, y_chips)
        return chip * 2 + lax.rem(core + dc, 2)

    order = sorted(range(y_chips), key=lambda d: (-min(d, y_chips - d), d))
    y_moves = [(dy, dc) for dy in order for dc in range(2) if (dy, dc) != (0, 0)]
    x_order = sorted(range(1, x_chips), key=lambda d: (-min(d, x_chips - d), d))

    def x_peer(sign, d):
        return zi * x_chips + lax.rem(xi + sign * d + x_chips, x_chips)

    def z_peer(sign, d):
        return lax.rem(zi + sign * d + z_chips, z_chips) * x_chips + xi

    barrier = pltpu.get_barrier_semaphore()
    for dy, dc in y_moves:
        pl.semaphore_signal(
            barrier, inc=1, device_id=(gxi, y_peer(1, dy, dc)), device_id_type=MESH
        )
    for d in x_order:
        pl.semaphore_signal(barrier, inc=1, device_id=(x_peer(1, d), gyi), device_id_type=MESH)
    for d in range(1, z_chips):
        pl.semaphore_signal(barrier, inc=1, device_id=(z_peer(1, d), gyi), device_id_type=MESH)

    def load(index, source, target):
        copy = pltpu.make_async_copy(source, target, table_sem.at[index])
        copy.start()
        return copy

    first_loads = [load(0, f_hbm, f_ref), load(1, c_hi_hbm, c_hi), load(2, c_lo_hbm, c_lo)]
    later_loads = [
        load(3, lines_hbm.at[gyi], lines), load(4, s_hi_hbm, s_hi), load(5, s_lo_hbm, s_lo),
    ]
    for copy in first_loads:
        copy.wait()

    for t in range(steps):
        cells = [
            [f_ref[pl.ds(2 * (t * sub + s) + b, lx, stride=ly), :] for s in range(sub)]
            for b in range(2)
        ]
        spread = jnp.concatenate([jnp.concatenate(row, axis=1) for row in cells], axis=0)
        high, low = split(spread)
        g_hi[t] = high
        g_lo[t] = low

    def block_of(index):
        return pl.ds(pl.multiple_of(index * block, block), block)

    def z_forward(c):
        for t in range(steps):
            piece = product((c_hi[c], c_lo[c]), (g_hi[t], g_lo[t]), ((1,), (1,)))
            for j in range(gy):
                out_fwd[c, j * block + t * TILE : j * block + (t + 1) * TILE, :] = piece[
                    j * TILE : (j + 1) * TILE, :
                ]

    def y_copies(c, out, into, send, recv):
        sends, arrivals = [], []
        for i, (dy, dc) in enumerate(y_moves):
            peer, source = y_peer(1, dy, dc), y_peer(-1, dy, dc)
            for copies, src, dst in ((sends, peer, gyi), (arrivals, source, source)):
                copies.append(
                    pltpu.make_async_remote_copy(
                        src_ref=out.at[c, block_of(src)],
                        dst_ref=into.at[c, block_of(dst)],
                        send_sem=send.at[c, i],
                        recv_sem=recv.at[c, i],
                        device_id=(gxi, peer),
                        device_id_type=MESH,
                    )
                )
        return sends, arrivals

    def exchange(c, out, into, send, recv):
        sends, arrivals = y_copies(c, out, into, send, recv)
        for copy in sends:
            copy.start()
        into[c, block_of(gyi), :] = out[c, block_of(gyi), :]
        return sends, arrivals

    z_forward(0)
    pl.semaphore_wait(barrier, len(y_moves) + x_chips - 1 + z_chips - 1)
    fwd = [exchange(0, out_fwd, in_fwd, fwd_send, fwd_recv)]
    for c in range(1, CHUNKS):
        z_forward(c)
        fwd.append(exchange(c, out_fwd, in_fwd, fwd_send, fwd_recv))

    for copy in later_loads:
        copy.wait()
    for c in range(CHUNKS):
        ratio = lines[c, 0]
        power = jnp.ones_like(ratio)
        for b in range(lx):
            powers[c, b] = power
            power = power * ratio

    def y_forward(c):
        for copy in fwd[c][1]:
            copy.wait_recv()
        tall = []
        for m in range(group):
            cells = jnp.concatenate(
                [in_fwd[c, pl.ds(s * group + m, part, stride=TILE), :] for s in range(sub)], axis=0
            ).T
            tall.append(jnp.concatenate([cells[:lx], cells[lx:]], axis=1))
        spectral = product(split(jnp.concatenate(tall, axis=0)), (s_hi[...], s_lo[...]),
                           ((1,), (0,)))
        for h in range(2):
            wave[c, h * group * lx : (h + 1) * group * lx, :] = spectral[:, h * ql : (h + 1) * ql]

    def small_copies(c, out, into, slot, send, recv, distances, peer_of, source_slot):
        sends, arrivals = [], []
        for i, d in enumerate(distances):
            for copies, dst in ((sends, slot), (arrivals, source_slot(d))):
                copies.append(
                    pltpu.make_async_remote_copy(
                        src_ref=out.at[c],
                        dst_ref=into.at[c, dst],
                        send_sem=send.at[c, i],
                        recv_sem=recv.at[c, i],
                        device_id=(peer_of(1, d), gyi),
                        device_id_type=MESH,
                    )
                )
        return sends, arrivals

    def line(ref, c, b):
        return ref[c, pl.ds(b, rows, stride=lx), :]

    def x_ends(c):
        left = [jnp.zeros((rows, ql), f32) for _ in range(4)]
        right = list(left)
        for b in range(lx):
            value = line(wave, c, b)
            left[b % 4] += value * powers[c, b]
            right[b % 4] += value * powers[c, lx - 1 - b]
        ends[c, :rows] = (left[0] + left[1]) + (left[2] + left[3])
        ends[c, rows:] = (right[0] + right[1]) + (right[2] + right[3])
        sends, arrivals = small_copies(
            c, ends, ends_x, xi, x_send, x_recv, x_order, x_peer,
            lambda d: lax.rem(xi - d + x_chips, x_chips),
        )
        for copy in sends:
            copy.start()
        ends_x[c, xi] = ends[c]
        return sends, arrivals

    def x_local(c):
        ratio = lines[c, 0]
        up = jnp.zeros((rows, ql), f32)
        down = up
        for b in range(lx):
            up = ratio * up + line(wave, c, b)
            sums_up[c, b] = up
            d = lx - 1 - b
            down = ratio * down
            sums_down[c, d] = down
            down = down + line(wave, c, d)

    def x_group(c, copies):
        for copy in copies[1]:
            copy.wait_recv()
        span = powers[c, lx - 1] * lines[c, 0]
        left = ends_x[c, x_chips - 1, :rows]
        right = ends_x[c, 0, rows:]
        for i in range(1, x_chips):
            left = span * left + ends_x[c, x_chips - 1 - i, :rows]
            right = span * right + ends_x[c, i, rows:]
        tops[c, :rows] = left
        tops[c, rows:] = right
        sends, arrivals = small_copies(
            c, tops, tops_z, zi, z_send, z_recv, range(1, z_chips), z_peer,
            lambda d: lax.rem(zi - d + z_chips, z_chips),
        )
        for copy in sends:
            copy.start()
        tops_z[c, zi] = tops[c]
        return sends, arrivals

    def arriving(c, span, count, place, parts, left_start, right_start):
        right = right_start
        left = left_start
        for i in range(count):
            left = jnp.where(i < place, span * left + parts[c, i, rows:], left)
            o = count - 1 - i
            right = jnp.where(o > place, span * right + parts[c, o, :rows], right)
        return left, right

    def x_finish(c, copies):
        ratio, scale = lines[c, 0], lines[c, 1]
        span = powers[c, lx - 1] * ratio
        wide = span
        for _ in range(x_chips - 1):
            wide = wide * span
        whole = wide
        for _ in range(z_chips - 1):
            whole = whole * wide
        for copy in copies[1]:
            copy.wait_recv()
        left = tops_z[c, z_chips - 1, :rows]
        right = tops_z[c, 0, rows:]
        for i in range(1, z_chips):
            left = wide * left + tops_z[c, z_chips - 1 - i, :rows]
            right = wide * right + tops_z[c, i, rows:]
        closing = 1.0 / (1.0 - whole * whole)
        first = (left + whole * right) * closing
        last = (right + whole * left) * closing
        first, last = arriving(c, wide, z_chips, zi, tops_z, first, last)
        first, last = arriving(c, span, x_chips, xi, ends_x, first, last)
        first = first * (ratio * scale)
        last = last * (ratio * scale)
        for b in range(lx):
            solved[c, pl.ds(b, rows, stride=lx), :] = (
                scale * (sums_up[c, b] + sums_down[c, b])
                + first * powers[c, b]
                + last * powers[c, lx - 1 - b]
            )

    def y_backward(c):
        flat = group * lx
        lanes = jnp.concatenate([solved[c, h * flat : (h + 1) * flat, :] for h in range(2)], axis=1)
        cells = product(split(lanes), (s_hi[...], s_lo[...]), ((1,), (1,)))
        for m in range(group):
            wide = cells[m * lx : (m + 1) * lx]
            tall = jnp.concatenate([wide[:, : ny // 2], wide[:, ny // 2 :]], axis=0).T
            for s in range(sub):
                out_bwd[c, pl.ds(s * group + m, part, stride=TILE), :] = tall[
                    s * part : (s + 1) * part
                ]
        return exchange(c, out_bwd, in_bwd, bwd_send, bwd_recv)

    def z_backward(c, copies):
        for copy in copies[1]:
            copy.wait_recv()
        for t in range(steps):
            waves = jnp.concatenate(
                [in_bwd[c, j * block + t * TILE : j * block + (t + 1) * TILE, :]
                 for j in range(gy)], axis=0,
            ).T
            cells = product(split(waves), (c_hi[c], c_lo[c]), ((1,), (0,)))
            if c > 0:
                cells = cells + total[t]
            if c < CHUNKS - 1:
                total[t] = cells
            else:
                for b in range(2):
                    for s in range(sub):
                        o_ref[pl.ds(2 * (t * sub + s) + b, lx, stride=ly), :] = cells[
                            b * lx : (b + 1) * lx, s * nz : (s + 1) * nz
                        ]

    x_copies, z_copies, bwd = {}, {}, {}

    def lines_out(c):
        y_forward(c)
        x_copies[c] = x_ends(c)
        x_local(c)

    def tops_out(c):
        z_copies[c] = x_group(c, x_copies[c])

    def back_out(c):
        x_finish(c, z_copies[c])
        bwd[c] = y_backward(c)

    for slot in range(CHUNKS + 3):
        if slot < CHUNKS:
            lines_out(slot)
        if 0 <= slot - 1 < CHUNKS:
            tops_out(slot - 1)
        if 0 <= slot - 2 < CHUNKS:
            back_out(slot - 2)
    for c in range(CHUNKS):
        z_backward(c, bwd[c])
    for sends, _ in [*fwd, *x_copies.values(), *z_copies.values(), *bwd.values()]:
        for copy in sends:
            copy.wait_send()


def solve(gx, gy, x_chips, source):
    lx, ly, nz = source.shape
    ny = ly * gy
    z_chips = gx // x_chips
    group = nz // gy // CHUNKS
    sub = TILE // group
    steps = ly // (2 * sub)
    rows, ql = 2 * group, ny // 2
    c_hi, c_lo = z_tables(nz, gy)
    s_hi, s_lo = y_tables(ny, gy, sub)
    lines = line_tables(ny, nz, gy)
    buffer = pltpu.VMEM((CHUNKS, gy * steps * TILE, 2 * lx), f32)
    spectral = pltpu.VMEM((CHUNKS, rows * lx, ql), f32)
    stack = pltpu.VMEM((CHUNKS, lx, rows, ql), f32)
    cells = pltpu.VMEM((steps, 2 * lx, sub * nz), bf16)
    dma = pltpu.SemaphoreType.DMA
    scratch = [
        pltpu.VMEM((lx * ly, nz), f32),
        pltpu.VMEM(c_hi.shape, bf16), pltpu.VMEM(c_lo.shape, bf16),
        pltpu.VMEM(s_hi.shape, bf16), pltpu.VMEM(s_lo.shape, bf16),
        pltpu.VMEM(lines.shape[1:], f32),
        cells, cells, buffer, buffer, spectral, stack, stack, stack, spectral, buffer, buffer,
        pltpu.VMEM((steps, 2 * lx, sub * nz), f32),
        pltpu.VMEM((CHUNKS, 2 * rows, ql), f32),
        pltpu.VMEM((CHUNKS, x_chips, 2 * rows, ql), f32),
        pltpu.VMEM((CHUNKS, 2 * rows, ql), f32),
        pltpu.VMEM((CHUNKS, z_chips, 2 * rows, ql), f32),
        dma((6,)),
        dma((CHUNKS, gy - 1)), dma((CHUNKS, gy - 1)), dma((CHUNKS, gy - 1)), dma((CHUNKS, gy - 1)),
        dma((CHUNKS, x_chips - 1)), dma((CHUNKS, x_chips - 1)),
        dma((CHUNKS, z_chips - 1)), dma((CHUNKS, z_chips - 1)),
    ]
    pressure = pl.pallas_call(
        functools.partial(kernel, gx, gy, x_chips, lx, ly, nz, ny),
        out_shape=pltpu.VMEM((lx * ly, nz), f32),
        in_specs=[pl.BlockSpec(memory_space=pl.ANY)] * 6,
        out_specs=pl.BlockSpec(memory_space=pltpu.VMEM),
        scratch_shapes=scratch,
        compiler_params=pltpu.CompilerParams(collective_id=0, has_side_effects=True),
    )(source.reshape(lx * ly, nz), c_hi, c_lo, s_hi, s_lo, lines)
    return pressure.reshape(lx, ly, nz)


def solution(mesh):
    gx, gy = mesh.shape["gx"], mesh.shape["gy"]
    return jax.shard_map(
        functools.partial(solve, gx, gy, X_CHIPS),
        mesh=mesh,
        in_specs=(P("gx", "gy", None),),
        out_specs=P("gx", "gy", None),
        check_vma=False,
    )
```

```python
import functools
import math

import jax
import jax.numpy as jnp
import ml_dtypes
import numpy as np
from jax import lax
from jax.experimental import pallas as pl
from jax.experimental.pallas import tpu as pltpu
from jax.sharding import PartitionSpec as P

SCREEN = 32
X_CHIPS = 4
CHUNKS = 4
TILE = 8
MESH = pl.DeviceIdType.MESH
f32, bf16 = jnp.float32, jnp.bfloat16


def halves(table):
    high = table.astype(ml_dtypes.bfloat16)
    low = (table - high.astype(np.float64)).astype(ml_dtypes.bfloat16)
    return high, low


def z_tables(nz, gy):
    waves, places = np.arange(nz)[:, None], np.arange(nz)[None, :]
    norm = np.where(waves == 0, math.sqrt(1.0 / nz), math.sqrt(2.0 / nz))
    cosines = norm * np.cos(np.pi * ((waves * (2 * places + 1)) % (4 * nz)) / (2 * nz))
    group = nz // gy // CHUNKS
    sub = TILE // group
    blocks = cosines.reshape(gy, CHUNKS, group, nz)
    table = np.zeros((CHUNKS, gy, sub, group, sub, nz))
    for s in range(sub):
        table[:, :, s, :, s, :] = blocks.transpose(1, 0, 2, 3)
    return halves(table.reshape(CHUNKS, gy * TILE, sub * nz))


def y_tables(ny, gy, sub):
    line = np.arange(1, ny + 1)
    sines = math.sqrt(2.0 / (ny + 1)) * np.sin(
        np.pi * ((line[:, None] * line[None, :]) % (2 * (ny + 1))) / (ny + 1)
    )
    cells = sines.reshape(gy, ny // gy // (2 * sub), sub, 2, ny)
    return halves(cells.transpose(3, 2, 0, 1, 4).reshape(ny, ny))


def line_tables(ny, nz, gy):
    q, m = np.arange(ny), np.arange(nz)
    shift = (
        1.0 / (SCREEN * SCREEN)
        + 4.0 * np.sin(np.pi * (q[:, None] + 1) / (2 * (ny + 1))) ** 2
        + 4.0 * np.sin(np.pi * m[None, :] / (2 * nz)) ** 2
    )
    root = np.sqrt(shift * (1.0 + shift / 4.0))
    ratio = 1.0 / (1.0 + shift / 2.0 + root)
    both = np.stack([ratio, 0.5 / root])
    group = nz // gy // CHUNKS
    both = both.reshape(2, 2, ny // 2, gy, CHUNKS, group)
    both = both.transpose(3, 4, 0, 1, 5, 2)
    return both.reshape(gy, CHUNKS, 2, 2 * group, ny // 2).astype(np.float32)


def split(value):
    high = value.astype(bf16)
    return high, (value - high.astype(f32)).astype(bf16)


def product(left, right, dims):
    def dot(a, b):
        return lax.dot_general(a, b, (dims, ((), ())), preferred_element_type=f32)

    return dot(left[0], right[0]) + (dot(left[1], right[0]) + dot(left[0], right[1]))


def kernel(
    gx, gy, x_chips, lx, ly, nz, ny,
    f_hbm, c_hi_hbm, c_lo_hbm, s_hi_hbm, s_lo_hbm, lines_hbm,
    o_ref,
    f_ref, c_hi, c_lo, s_hi, s_lo, lines,
    g_hi, g_lo, out_fwd, in_fwd, wave, powers, sums_up, sums_down, solved, out_bwd, in_bwd, total,
    ends, ends_x, tops, tops_z,
    table_sem, fwd_send, fwd_recv, bwd_send, bwd_recv, x_send, x_recv, z_send, z_recv,
):
    z_chips, y_chips = gx // x_chips, gy // 2
    group = nz // gy // CHUNKS
    sub = TILE // group
    steps = ly // (2 * sub)
    rows = 2 * group
    block = steps * TILE
    part = gy * steps
    ql = ny // 2

    gxi, gyi = lax.axis_index("gx"), lax.axis_index("gy")
    zi, xi = gxi // x_chips, lax.rem(gxi, x_chips)
    yi, core = gyi // 2, lax.rem(gyi, 2)

    def y_peer(sign, dy, dc):
        chip = lax.rem(yi + sign * dy + y_chips, y_chips)
        return chip * 2 + lax.rem(core + dc, 2)

    order = sorted(range(y_chips), key=lambda d: (-min(d, y_chips - d), d))
    y_moves = [(dy, dc) for dy in order for dc in range(2) if (dy, dc) != (0, 0)]
    x_order = sorted(range(1, x_chips), key=lambda d: (-min(d, x_chips - d), d))

    def x_peer(sign, d):
        return zi * x_chips + lax.rem(xi + sign * d + x_chips, x_chips)

    def z_peer(sign, d):
        return lax.rem(zi + sign * d + z_chips, z_chips) * x_chips + xi

    barrier = pltpu.get_barrier_semaphore()
    for dy, dc in y_moves:
        pl.semaphore_signal(
            barrier, inc=1, device_id=(gxi, y_peer(1, dy, dc)), device_id_type=MESH
        )
    for d in x_order:
        pl.semaphore_signal(barrier, inc=1, device_id=(x_peer(1, d), gyi), device_id_type=MESH)
    for d in range(1, z_chips):
        pl.semaphore_signal(barrier, inc=1, device_id=(z_peer(1, d), gyi), device_id_type=MESH)

    def load(index, source, target):
        copy = pltpu.make_async_copy(source, target, table_sem.at[index])
        copy.start()
        return copy

    first_loads = [load(0, f_hbm, f_ref), load(1, c_hi_hbm, c_hi), load(2, c_lo_hbm, c_lo)]
    later_loads = [
        load(3, lines_hbm.at[gyi], lines), load(4, s_hi_hbm, s_hi), load(5, s_lo_hbm, s_lo),
    ]
    for copy in first_loads:
        copy.wait()

    for t in range(steps):
        cells = [
            [f_ref[pl.ds(2 * (t * sub + s) + b, lx, stride=ly), :] for s in range(sub)]
            for b in range(2)
        ]
        spread = jnp.concatenate([jnp.concatenate(row, axis=1) for row in cells], axis=0)
        high, low = split(spread)
        g_hi[t] = high
        g_lo[t] = low

    def block_of(index):
        return pl.ds(pl.multiple_of(index * block, block), block)

    def z_forward(c):
        for t in range(steps):
            piece = product((c_hi[c], c_lo[c]), (g_hi[t], g_lo[t]), ((1,), (1,)))
            for j in range(gy):
                out_fwd[c, j * block + t * TILE : j * block + (t + 1) * TILE, :] = piece[
                    j * TILE : (j + 1) * TILE, :
                ]

    def y_copies(c, out, into, send, recv):
        sends, arrivals = [], []
        for i, (dy, dc) in enumerate(y_moves):
            peer, source = y_peer(1, dy, dc), y_peer(-1, dy, dc)
            for copies, src, dst in ((sends, peer, gyi), (arrivals, source, source)):
                copies.append(
                    pltpu.make_async_remote_copy(
                        src_ref=out.at[c, block_of(src)],
                        dst_ref=into.at[c, block_of(dst)],
                        send_sem=send.at[c, i],
                        recv_sem=recv.at[c, i],
                        device_id=(gxi, peer),
                        device_id_type=MESH,
                    )
                )
        return sends, arrivals

    def exchange(c, out, into, send, recv):
        sends, arrivals = y_copies(c, out, into, send, recv)
        for copy in sends:
            copy.start()
        into[c, block_of(gyi), :] = out[c, block_of(gyi), :]
        return sends, arrivals

    z_forward(0)
    pl.semaphore_wait(barrier, len(y_moves) + x_chips - 1 + z_chips - 1)
    fwd = [exchange(0, out_fwd, in_fwd, fwd_send, fwd_recv)]
    for c in range(1, CHUNKS):
        z_forward(c)
        fwd.append(exchange(c, out_fwd, in_fwd, fwd_send, fwd_recv))

    for copy in later_loads:
        copy.wait()
    for c in range(CHUNKS):
        ratio = lines[c, 0]
        power = jnp.ones_like(ratio)
        for b in range(lx):
            powers[c, b] = power
            power = power * ratio

    def y_forward(c):
        for copy in fwd[c][1]:
            copy.wait_recv()
        tall = []
        for m in range(group):
            cells = jnp.concatenate(
                [in_fwd[c, pl.ds(s * group + m, part, stride=TILE), :] for s in range(sub)], axis=0
            ).T
            tall.append(jnp.concatenate([cells[:lx], cells[lx:]], axis=1))
        spectral = product(split(jnp.concatenate(tall, axis=0)), (s_hi[...], s_lo[...]),
                           ((1,), (0,)))
        for h in range(2):
            wave[c, h * group * lx : (h + 1) * group * lx, :] = spectral[:, h * ql : (h + 1) * ql]

    def small_copies(c, out, into, slot, send, recv, distances, peer_of, source_slot):
        sends, arrivals = [], []
        for i, d in enumerate(distances):
            for copies, dst in ((sends, slot), (arrivals, source_slot(d))):
                copies.append(
                    pltpu.make_async_remote_copy(
                        src_ref=out.at[c],
                        dst_ref=into.at[c, dst],
                        send_sem=send.at[c, i],
                        recv_sem=recv.at[c, i],
                        device_id=(peer_of(1, d), gyi),
                        device_id_type=MESH,
                    )
                )
        return sends, arrivals

    def line(ref, c, b):
        return ref[c, pl.ds(b, rows, stride=lx), :]

    def x_ends(c):
        left = [jnp.zeros((rows, ql), f32) for _ in range(4)]
        right = list(left)
        for b in range(lx):
            value = line(wave, c, b)
            left[b % 4] += value * powers[c, b]
            right[b % 4] += value * powers[c, lx - 1 - b]
        ends[c, :rows] = (left[0] + left[1]) + (left[2] + left[3])
        ends[c, rows:] = (right[0] + right[1]) + (right[2] + right[3])
        sends, arrivals = small_copies(
            c, ends, ends_x, xi, x_send, x_recv, x_order, x_peer,
            lambda d: lax.rem(xi - d + x_chips, x_chips),
        )
        for copy in sends:
            copy.start()
        ends_x[c, xi] = ends[c]
        return sends, arrivals

    def x_local(c):
        ratio = lines[c, 0]
        up = jnp.zeros((rows, ql), f32)
        down = up
        for b in range(lx):
            up = ratio * up + line(wave, c, b)
            sums_up[c, b] = up
            d = lx - 1 - b
            down = ratio * down
            sums_down[c, d] = down
            down = down + line(wave, c, d)

    def x_group(c, copies):
        for copy in copies[1]:
            copy.wait_recv()
        span = powers[c, lx - 1] * lines[c, 0]
        left = ends_x[c, x_chips - 1, :rows]
        right = ends_x[c, 0, rows:]
        for i in range(1, x_chips):
            left = span * left + ends_x[c, x_chips - 1 - i, :rows]
            right = span * right + ends_x[c, i, rows:]
        tops[c, :rows] = left
        tops[c, rows:] = right
        sends, arrivals = small_copies(
            c, tops, tops_z, zi, z_send, z_recv, range(1, z_chips), z_peer,
            lambda d: lax.rem(zi - d + z_chips, z_chips),
        )
        for copy in sends:
            copy.start()
        tops_z[c, zi] = tops[c]
        return sends, arrivals

    def arriving(c, span, count, place, parts, left_start, right_start):
        right = right_start
        left = left_start
        for i in range(count):
            left = jnp.where(i < place, span * left + parts[c, i, rows:], left)
            o = count - 1 - i
            right = jnp.where(o > place, span * right + parts[c, o, :rows], right)
        return left, right

    def x_finish(c, copies):
        ratio, scale = lines[c, 0], lines[c, 1]
        span = powers[c, lx - 1] * ratio
        wide = span
        for _ in range(x_chips - 1):
            wide = wide * span
        whole = wide
        for _ in range(z_chips - 1):
            whole = whole * wide
        for copy in copies[1]:
            copy.wait_recv()
        left = tops_z[c, z_chips - 1, :rows]
        right = tops_z[c, 0, rows:]
        for i in range(1, z_chips):
            left = wide * left + tops_z[c, z_chips - 1 - i, :rows]
            right = wide * right + tops_z[c, i, rows:]
        closing = 1.0 / (1.0 - whole * whole)
        first = (left + whole * right) * closing
        last = (right + whole * left) * closing
        first, last = arriving(c, wide, z_chips, zi, tops_z, first, last)
        first, last = arriving(c, span, x_chips, xi, ends_x, first, last)
        first = first * (ratio * scale)
        last = last * (ratio * scale)
        for b in range(lx):
            solved[c, pl.ds(b, rows, stride=lx), :] = (
                scale * (sums_up[c, b] + sums_down[c, b])
                + first * powers[c, b]
                + last * powers[c, lx - 1 - b]
            )

    def y_backward(c):
        flat = group * lx
        lanes = jnp.concatenate([solved[c, h * flat : (h + 1) * flat, :] for h in range(2)], axis=1)
        cells = product(split(lanes), (s_hi[...], s_lo[...]), ((1,), (1,)))
        for m in range(group):
            wide = cells[m * lx : (m + 1) * lx]
            tall = jnp.concatenate([wide[:, : ny // 2], wide[:, ny // 2 :]], axis=0).T
            for s in range(sub):
                out_bwd[c, pl.ds(s * group + m, part, stride=TILE), :] = tall[
                    s * part : (s + 1) * part
                ]
        return exchange(c, out_bwd, in_bwd, bwd_send, bwd_recv)

    def z_backward(c, copies):
        for copy in copies[1]:
            copy.wait_recv()
        for t in range(steps):
            waves = jnp.concatenate(
                [in_bwd[c, j * block + t * TILE : j * block + (t + 1) * TILE, :]
                 for j in range(gy)], axis=0,
            ).T
            cells = product(split(waves), (c_hi[c], c_lo[c]), ((1,), (0,)))
            if c > 0:
                cells = cells + total[t]
            if c < CHUNKS - 1:
                total[t] = cells
            else:
                for b in range(2):
                    for s in range(sub):
                        o_ref[pl.ds(2 * (t * sub + s) + b, lx, stride=ly), :] = cells[
                            b * lx : (b + 1) * lx, s * nz : (s + 1) * nz
                        ]

    x_copies, z_copies, bwd = {}, {}, {}

    def lines_out(c):
        y_forward(c)
        x_copies[c] = x_ends(c)
        x_local(c)

    def tops_out(c):
        z_copies[c] = x_group(c, x_copies[c])

    def back_out(c):
        x_finish(c, z_copies[c])
        bwd[c] = y_backward(c)

    for slot in range(CHUNKS + 3):
        if slot < CHUNKS:
            lines_out(slot)
        if 0 <= slot - 1 < CHUNKS:
            tops_out(slot - 1)
        if 0 <= slot - 2 < CHUNKS:
            back_out(slot - 2)
    for c in range(CHUNKS):
        z_backward(c, bwd[c])
    for sends, _ in [*fwd, *x_copies.values(), *z_copies.values(), *bwd.values()]:
        for copy in sends:
            copy.wait_send()


def solve(gx, gy, x_chips, source):
    lx, ly, nz = source.shape
    ny = ly * gy
    z_chips = gx // x_chips
    group = nz // gy // CHUNKS
    sub = TILE // group
    steps = ly // (2 * sub)
    rows, ql = 2 * group, ny // 2
    c_hi, c_lo = z_tables(nz, gy)
    s_hi, s_lo = y_tables(ny, gy, sub)
    lines = line_tables(ny, nz, gy)
    buffer = pltpu.VMEM((CHUNKS, gy * steps * TILE, 2 * lx), f32)
    spectral = pltpu.VMEM((CHUNKS, rows * lx, ql), f32)
    stack = pltpu.VMEM((CHUNKS, lx, rows, ql), f32)
    cells = pltpu.VMEM((steps, 2 * lx, sub * nz), bf16)
    dma = pltpu.SemaphoreType.DMA
    scratch = [
        pltpu.VMEM((lx * ly, nz), f32),
        pltpu.VMEM(c_hi.shape, bf16), pltpu.VMEM(c_lo.shape, bf16),
        pltpu.VMEM(s_hi.shape, bf16), pltpu.VMEM(s_lo.shape, bf16),
        pltpu.VMEM(lines.shape[1:], f32),
        cells, cells, buffer, buffer, spectral, stack, stack, stack, spectral, buffer, buffer,
        pltpu.VMEM((steps, 2 * lx, sub * nz), f32),
        pltpu.VMEM((CHUNKS, 2 * rows, ql), f32),
        pltpu.VMEM((CHUNKS, x_chips, 2 * rows, ql), f32),
        pltpu.VMEM((CHUNKS, 2 * rows, ql), f32),
        pltpu.VMEM((CHUNKS, z_chips, 2 * rows, ql), f32),
        dma((6,)),
        dma((CHUNKS, gy - 1)), dma((CHUNKS, gy - 1)), dma((CHUNKS, gy - 1)), dma((CHUNKS, gy - 1)),
        dma((CHUNKS, x_chips - 1)), dma((CHUNKS, x_chips - 1)),
        dma((CHUNKS, z_chips - 1)), dma((CHUNKS, z_chips - 1)),
    ]
    pressure = pl.pallas_call(
        functools.partial(kernel, gx, gy, x_chips, lx, ly, nz, ny),
        out_shape=pltpu.VMEM((lx * ly, nz), f32),
        in_specs=[pl.BlockSpec(memory_space=pl.ANY)] * 6,
        out_specs=pl.BlockSpec(memory_space=pltpu.VMEM),
        scratch_shapes=scratch,
        compiler_params=pltpu.CompilerParams(collective_id=0, has_side_effects=True),
    )(source.reshape(lx * ly, nz), c_hi, c_lo, s_hi, s_lo, lines)
    return pressure.reshape(lx, ly, nz)


def solution(mesh):
    gx, gy = mesh.shape["gx"], mesh.shape["gy"]
    return jax.shard_map(
        functools.partial(solve, gx, gy, X_CHIPS),
        mesh=mesh,
        in_specs=(P("gx", "gy", None),),
        out_specs=P("gx", "gy", None),
        check_vma=False,
    )
```
